32 devices in a mesh: groups: 2 (over y), space: 8 (over z, x), tm: 2 (over core).
Axes of the slice: x: 2, y: 2, z: 4, core: 2. Of those that a mesh axis runs over, the one named last changes fastest.
Arguments:
- base_latent: bfloat16 [64, 2, 12, 128], P(('groups', 'space'), 'tm'), parts along dimension 0, may hold values from -6 to 6
- cotangent: bfloat16 [64, 8, 48, 128], P(('groups', 'space'), 'tm'), parts along dimension 0, may hold values from -6 to 6
- w_spatial: bfloat16 [3, 3, 128, 128], replicated, may hold values from -0.1875 to 0.1875
- w_temporal: bfloat16 [5, 128, 128], replicated, may hold values from -0.25 to 0.25
Outputs:
- result: bfloat16 [64, 8, 48, 128], P(('groups', 'space'), 'tm'), parts along dimension 0
- grad_base: float32 [64, 2, 12, 128], P(('groups', 'space'), 'tm'), parts along dimension 0
- grad_spatial: float32 [6, 3, 128, 128], P('groups'), parts along dimension 0
- grad_temporal: float32 [10, 128, 128], P('groups'), parts along dimension 0
The draws below stay inside these ranges and needn't reach their ends.
There are 2 independent parts, one for each index of `groups`. The reference program is written for one: setup_inputs(seed, part) draws one part's arguments, and reference() takes and returns one part's arrays. A program takes and returns all parts, laid end to end along the dimension named above; an argument that names none is the same for every part. Nothing has to cross between parts.
All inputs are finite; a program needn't handle non-finite values.
Results may differ from the reference program's by a relative error of at most 0.0064.
Values may be sent and summed in bfloat16 or wider, within the bound.
No kernel may reach another device: no remote copies, remote signals or barrier semaphores. Data moves between devices by JAX's collectives and lax.ppermute only.
A program may use at most 64 MiB of HBM per device.

```python
import jax
import jax.numpy as jnp
from jax import lax

C = 128
W = 48
FRAME_DILATION = 2
F = 32
H = 8
LH = 2
LW = 12


def shard_levels(stream_key, shape, shards, low, largest):
    level, own = 1.0, jax.random.fold_in(stream_key, 6)
    for axis_at, parts in shards:
        draws = jnp.exp(jax.random.uniform(jax.random.fold_in(own, axis_at), (parts,), jnp.float32, low / len(shards), largest / len(shards)))
        level = level * jnp.repeat(draws, shape[axis_at] // parts).reshape([-1 if axis == axis_at else 1 for axis in range(len(shape))])
    return level


def scatter_about(key, extent, width, limit, pieces=(), dtype=jnp.bfloat16):
    values = jax.random.normal(key, extent, jnp.float32) * width
    if len(pieces) > 0:
        values = shard_levels(key, extent, pieces, -0.22, 0.18) * values
    return jnp.clip(values, min=-limit, max=limit).astype(dtype)


def setup_inputs(seed: int = 0, part: int = 0) -> dict:
    streams_of = jax.random.split(jax.random.key(seed), 5)
    part_splits = jax.random.split(jax.random.fold_in(streams_of[4], part), 5)
    base_latent = scatter_about(part_splits[0], (F, LH, LW, C), 1.0, 6.0, ((0, 8), (1, 2)))
    cotangent = scatter_about(part_splits[1], (F, H, W, C), 1.0, 6.0, ((0, 8), (1, 2)))
    w_spatial = scatter_about(streams_of[2], (3, 3, C, C), (9 * C) ** -0.5, 0.1875)
    w_temporal = scatter_about(streams_of[3], (5, C, C), (5 * C) ** -0.5, 0.25)
    return {"base_latent": base_latent, "cotangent": cotangent, "w_spatial": w_spatial, "w_temporal": w_temporal}


def widen_cols(field):
    left_cols = jnp.concatenate([field[:, :, :1], field[:, :, :-1]], axis=2)
    right_cols = jnp.concatenate([field[:, :, 1:], field[:, :, -1:]], axis=2)
    phases = jnp.stack([0.375 * left_cols + 0.625 * field, 0.125 * left_cols + 0.875 * field, 0.875 * field + 0.125 * right_cols, 0.625 * field + 0.375 * right_cols], axis=3)
    return phases.reshape(field.shape[0], field.shape[1], field.shape[2] * 4, field.shape[3])

def widen_rows(below_rows, middle, above_rows):
    phases = jnp.stack([0.375 * below_rows + 0.625 * middle, 0.125 * below_rows + 0.875 * middle, 0.875 * middle + 0.125 * above_rows, 0.625 * middle + 0.375 * above_rows], axis=2)
    return phases.reshape(middle.shape[0], middle.shape[1] * 4, middle.shape[2], middle.shape[3])

def upsample(latent):
    below_rows = jnp.concatenate([latent[:, :1], latent[:, :-1]], axis=1)
    above_rows = jnp.concatenate([latent[:, 1:], latent[:, -1:]], axis=1)
    return widen_cols(widen_rows(below_rows, latent, above_rows))

def silu_slope(value):
    sigmoid_val = jax.nn.sigmoid(value)
    return sigmoid_val * (1.0 + value * (1.0 - sigmoid_val))

def conv_three(padded, weight, row_count, col_count, start):
    frame_count = padded.shape[0]
    channels = weight.shape[3]
    summed = jnp.zeros((frame_count * row_count * col_count, channels), jnp.float32)
    for tap_row in range(3):
        for tap_col in range(3):
            r0 = start - tap_row if start else tap_row
            c0 = start - tap_col if start else tap_col
            frame_window = padded[:, r0:r0 + row_count, c0:c0 + col_count].reshape(-1, padded.shape[3])
            kernel = weight[tap_row, tap_col] if not start else weight[tap_row, tap_col].T
            summed = summed + jnp.dot(frame_window, kernel, preferred_element_type=jnp.float32)
    return summed.reshape(frame_count, row_count, col_count, channels)

def space_grads(padded, delta, row_count, col_count):
    flat = delta.reshape(-1, delta.shape[3])
    taps = []
    for tap_row in range(3):
        for tap_col in range(3):
            frame_window = padded[:, tap_row:tap_row + row_count, tap_col:tap_col + col_count].reshape(-1, padded.shape[3])
            taps.append(lax.dot_general(frame_window, flat, (((0,), (0,)), ((), ())), preferred_element_type=jnp.float32))
    return jnp.stack(taps).reshape(3, 3, padded.shape[3], delta.shape[3])

def conv_time(frames_extended, weight, frame_count, reversed_order):
    channels = weight.shape[2]
    tensor_shape = frames_extended.shape
    summed = jnp.zeros((frame_count * tensor_shape[1] * tensor_shape[2], channels), jnp.float32)
    for kernel_tap in range(5):
        frame_offset = (4 - kernel_tap) * FRAME_DILATION if reversed_order else kernel_tap * FRAME_DILATION
        frame_window = frames_extended[frame_offset:frame_offset + frame_count].reshape(-1, tensor_shape[3])
        kernel = weight[kernel_tap].T if reversed_order else weight[kernel_tap]
        summed = summed + jnp.dot(frame_window, kernel, preferred_element_type=jnp.float32)
    return summed.reshape(frame_count, tensor_shape[1], tensor_shape[2], channels)

def time_grads(frames_extended, delta, frame_count):
    flat = delta.reshape(-1, delta.shape[3])
    taps = []
    for kernel_tap in range(5):
        frame_window = frames_extended[kernel_tap * FRAME_DILATION:kernel_tap * FRAME_DILATION + frame_count].reshape(-1, frames_extended.shape[3])
        taps.append(lax.dot_general(frame_window, flat, (((0,), (0,)), ((), ())), preferred_element_type=jnp.float32))
    return jnp.stack(taps)

def reference(base_latent, cotangent, w_spatial, w_temporal):
    upsampled = upsample(base_latent.astype(jnp.float32)).astype(jnp.bfloat16)
    frame_count, row_count, col_count = (upsampled.shape[0], upsampled.shape[1], upsampled.shape[2])
    padded = jnp.pad(upsampled, ((0, 0), (1, 1), (1, 1), (0, 0)))
    pre_one = conv_three(padded, w_spatial, row_count, col_count, 0)
    first_activation = jax.nn.silu(pre_one).astype(jnp.bfloat16)
    frames_extended = jnp.pad(first_activation, ((2 * FRAME_DILATION, 2 * FRAME_DILATION), (0, 0), (0, 0), (0, 0)))
    pre_two = conv_time(frames_extended, w_temporal, frame_count, False)
    result = (upsampled.astype(jnp.float32) + jax.nn.silu(pre_two)).astype(jnp.bfloat16)
    upstream = cotangent.astype(jnp.float32)
    second_gradient = (upstream * silu_slope(pre_two)).astype(jnp.bfloat16)
    grad_temporal = time_grads(frames_extended, second_gradient, frame_count)
    gradient_extended = jnp.pad(second_gradient, ((2 * FRAME_DILATION, 2 * FRAME_DILATION), (0, 0), (0, 0), (0, 0)))
    back_one = conv_time(gradient_extended, w_temporal, frame_count, True)
    delta_one = (back_one * silu_slope(pre_one)).astype(jnp.bfloat16)
    grad_spatial = space_grads(padded, delta_one, row_count, col_count)
    delta_pad = jnp.pad(delta_one, ((0, 0), (1, 1), (1, 1), (0, 0)))
    grad_image = upstream + conv_three(delta_pad, w_spatial, row_count, col_count, 2)
    _, pullback = jax.vjp(upsample, base_latent.astype(jnp.float32))
    grad_base = pullback(grad_image)[0]
    return (result, grad_base, grad_spatial, grad_temporal)
```

```python
import jax
import jax.numpy as jnp
import numpy as np
from jax import lax
from jax.experimental import pallas as pl
from jax.experimental.pallas import tpu as pltpu
from jax.sharding import PartitionSpec as P

BF = jnp.bfloat16
F32 = jnp.float32
C = 128
FRAMES = 4
ROWS = 4
COLS = 48
LROWS = 2
LCOLS = 12
PIX = ROWS * COLS
LOW = LROWS * LCOLS
TAPS = 9
LT = TAPS * LOW
GROUP = 2 * PIX
BOTH = ("space", "tm")


def up_matrix(n):
    m = np.zeros((4 * n, n))
    for k in range(n):
        lo, hi = max(k - 1, 0), min(k + 1, n - 1)
        for j, (a, at) in enumerate(((0.375, lo), (0.125, lo), (0.125, hi), (0.375, hi))):
            m[4 * k + j, at] += a
            m[4 * k + j, k] += 1.0 - a
    return m


def moved(m, tap):
    out = np.zeros_like(m)
    for i in range(m.shape[0]):
        if 0 <= i + tap - 1 < m.shape[0]:
            out[i] = m[i + tap - 1]
    return out


def constants():
    rows, cols = up_matrix(LROWS), up_matrix(LCOLS)
    up = np.kron(rows, cols).reshape(2, PIX, LOW)
    conv = np.concatenate(
        [np.kron(moved(rows, a), moved(cols, b)) for a in range(3) for b in range(3)], axis=1
    ).reshape(2, PIX, LT)
    as_bf = lambda m: jnp.asarray(m, BF)
    return as_bf(up), as_bf(conv), as_bf(up.transpose(0, 2, 1)), as_bf(conv.transpose(0, 2, 1))


def dot(a, b, dims=((1,), (0,))):
    return lax.dot_general(a, b, (dims, ((), ())), preferred_element_type=F32)


def lanes(parts):
    return jnp.concatenate(parts, axis=1)


def forward_kernel(
    base, near, far_near, cot, conv, up, ws, wt, res, gt, d2, slope1, slope2, z, act
):
    core = lax.axis_index("tm")
    at = lax.axis_index("space")
    count = lax.axis_size("space")

    def low_res(block, slot):
        for tap in range(TAPS):
            prod = dot(block, ws[tap]).reshape(FRAMES, LOW, C)
            z[pl.ds(slot * FRAMES, FRAMES), tap * LOW : (tap + 1) * LOW, :] = prod

    low_res(base[...], 2)
    mine_back = core == 0
    for ref, back in ((near, mine_back), (far_near, jnp.logical_not(mine_back))):
        for hop in (1, 2):
            inside = jnp.where(back, at - hop >= 0, at + hop < count)
            block = ref[(hop - 1) * FRAMES * LOW : hop * FRAMES * LOW, :]
            block = jnp.where(inside, block, jnp.zeros_like(block))
            low_res(block, jnp.where(back, 2 - hop, 2 + hop))

    matrix = conv[core]
    for p in range(5 * FRAMES // 2):
        pair = lanes([z[2 * p], z[2 * p + 1]]).astype(BF)
        pre = dot(matrix, pair)
        sig = jax.nn.sigmoid(pre)
        one = (pre * sig).astype(BF)
        for k in range(2):
            act[p * GROUP + k * PIX : p * GROUP + (k + 1) * PIX, :] = one[:, k * C : (k + 1) * C]
        if p in (4, 5):
            slope = sig * (1.0 + pre * (1.0 - sig))
            for k in range(2):
                lo = (p - 4) * GROUP + k * PIX
                slope1[lo : lo + PIX, :] = slope[:, k * C : (k + 1) * C]

    zero = jnp.zeros((C, C), BF)
    time = jnp.concatenate(
        [
            lanes([wt[k] if k < 5 else zero, wt[k - 1] if k > 0 else zero])
            for k in range(6)
        ],
        axis=0,
    )

    def window(first):
        return lanes([act[(first + k) * GROUP : (first + k + 1) * GROUP, :] for k in range(6)])

    def time_conv(first):
        pre = dot(window(first), time)
        sig = jax.nn.sigmoid(pre)
        return pre, sig, sig * (1.0 + pre * (1.0 - sig))

    pre, sig, slope = time_conv(2)
    extra = pre * sig
    upm = up[core]
    for p in range(2):
        for k in range(2):
            f = 2 * p + k
            big = dot(upm, base[f * LOW : (f + 1) * LOW, :]).astype(BF).astype(F32)
            res[f * PIX : (f + 1) * PIX, :] = (
                big + extra[k * PIX : (k + 1) * PIX, p * C : (p + 1) * C]
            ).astype(BF)
        lo = p * GROUP
        d2[lo : lo + GROUP, :] = (
            cot[lo : lo + GROUP, :].astype(F32) * slope[:, p * C : (p + 1) * C]
        ).astype(BF)
    for side, first in ((0, 0), (1, 4)):
        slope = time_conv(first)[2]
        for p in range(2):
            slope2[side, p * GROUP : (p + 1) * GROUP, :] = slope[:, p * C : (p + 1) * C]

    outer = dot(window(2), lanes([d2[:GROUP, :], d2[GROUP:, :]]), ((0,), (0,)))
    for t in range(5):
        gt[t] = outer[t * C : (t + 1) * C, :C] + outer[(t + 1) * C : (t + 2) * C, C:]


def backward_kernel(
    even, odd, d2, slope1, slope2, cot, base, gt, conv_t, up_t, ws, wt, send, keep, low, dsc
):
    core = lax.axis_index("tm")
    at = lax.axis_index("space")
    count = lax.axis_size("space")
    is_even = at % 2 == 0
    zeros = jnp.zeros((FRAMES * PIX, C), F32)

    def outside(first, second, inside, side):
        got = jnp.where(is_even, first[...], second[...]).astype(F32)
        return jnp.where(inside, (got * slope2[side]), zeros).astype(BF)

    before = outside(odd, even, at > 0, 0)
    after = outside(even, odd, at < count - 1, 1)
    window = lanes(
        [
            before[:GROUP],
            before[GROUP:],
            d2[:GROUP, :],
            d2[GROUP:, :],
            after[:GROUP],
            after[GROUP:],
        ]
    )
    zero = jnp.zeros((C, C), BF)
    time = jnp.concatenate(
        [
            lanes([wt[4 - k] if k < 5 else zero for k in range(6)]),
            lanes([wt[5 - k] if k > 0 else zero for k in range(6)]),
        ],
        axis=0,
    )
    back = dot(window, time, ((1,), (1,)))
    matrix = conv_t[core]
    for p in range(2):
        lo = p * GROUP
        d1 = (back[:, p * C : (p + 1) * C] * slope1[lo : lo + GROUP, :]).astype(BF)
        small = dot(matrix, lanes([d1[:PIX], d1[PIX:]]))
        dsc[2 * p] = small[:, :C]
        dsc[2 * p + 1] = small[:, C:]
    taps = [
        dsc[:, k * LOW : (k + 1) * LOW, :].reshape(FRAMES * LOW, C).astype(BF) for k in range(TAPS)
    ]
    every = lanes(taps)
    total = dot(every, lanes([ws[k] for k in range(TAPS)]), ((1,), (1,)))
    direct = dot(up_t[core], lanes([cot[f * PIX : (f + 1) * PIX, :] for f in range(FRAMES)]))
    for f in range(FRAMES):
        low[f * LOW : (f + 1) * LOW, :] = (
            total[f * LOW : (f + 1) * LOW, :] + direct[:, f * C : (f + 1) * C]
        )
    space = dot(base[...], every, ((0,), (0,)))
    grads = [space[:, k * C : (k + 1) * C] for k in range(TAPS)] + [gt[t] for t in range(5)]
    for j in range(7):
        first, second = grads[j], grads[j + 7]
        send[j] = jnp.where(core == 0, second, first).astype(send.dtype)
        keep[j] = jnp.where(core == 0, first, second)


def full(pairs, total):
    sources, targets = {a for a, _ in pairs}, {b for _, b in pairs}
    return pairs + list(
        zip(
            [i for i in range(total) if i not in sources],
            [i for i in range(total) if i not in targets],
        )
    )


def hop_pairs(count, hop):
    pairs = []
    for s in range(count):
        pairs.append((2 * s, 2 * (s + hop)) if s + hop < count else (2 * s, 2 * s + 1))
        pairs.append((2 * s + 1, 2 * (s - hop) + 1) if s - hop >= 0 else (2 * s + 1, 2 * s))
    return pairs


def swap_pairs(count, first):
    pairs = []
    for i in range(first, count - 1, 2):
        pairs += [(i, i + 1), (i + 1, i)]
    return full(pairs, count)


def swap_cores(value):
    return lax.ppermute(value, "tm", [(0, 1), (1, 0)])


def reduce_chips(value, count, core, at):
    bits = count.bit_length() - 1
    if count != 1 << bits:
        return lax.psum(value, "space").astype(BF)
    orders = [list(range(bits)), [(b + 2) % bits for b in range(bits)]] if bits > 2 else [list(range(bits))] * 2

    def pairs_of(step):
        pairs = []
        for s in range(count):
            for c in range(2):
                pairs.append((2 * s + c, 2 * (s ^ (1 << orders[c][step])) + c))
        return pairs

    def bit_of(step):
        return jnp.where(core == 0, (at >> orders[0][step]) & 1, (at >> orders[1][step]) & 1)

    levels = min(1, bits)
    for step in range(levels):
        halves = value.reshape(2, value.shape[0] // 2, C)
        bit = bit_of(step)
        out = lax.dynamic_index_in_dim(halves, 1 - bit, 0, False).astype(BF)
        mine = lax.dynamic_index_in_dim(halves, bit, 0, False)
        value = mine + lax.ppermute(out, BOTH, pairs_of(step)).astype(F32)
    for step in range(levels, bits):
        out = value.astype(BF)
        value = out.astype(F32) + lax.ppermute(out, BOTH, pairs_of(step)).astype(F32)
    value = value.astype(BF)
    for step in reversed(range(levels)):
        got = lax.ppermute(value, BOTH, pairs_of(step))
        value = jnp.where(
            bit_of(step) == 0,
            jnp.concatenate([value, got], axis=0),
            jnp.concatenate([got, value], axis=0),
        )
    return value


def local(base_latent, cotangent, w_spatial, w_temporal):
    core = lax.axis_index("tm")
    at = lax.axis_index("space")
    count = lax.axis_size("space")
    up, conv, up_t, conv_t = constants()
    ws = w_spatial.reshape(TAPS, C, C)
    cot = cotangent.reshape(FRAMES * PIX, C)
    own = base_latent.reshape(FRAMES, LCOLS, C)
    other = swap_cores(own)
    base = jnp.where(
        core == 0, jnp.concatenate([own, other], axis=1), jnp.concatenate([other, own], axis=1)
    ).reshape(FRAMES * LOW, C)
    near = jnp.concatenate(
        [lax.ppermute(base, BOTH, hop_pairs(count, hop)) for hop in (1, 2)], axis=0
    )
    far = swap_cores(near)
    even = lax.ppermute(cot, "space", swap_pairs(count, 0))
    odd = lax.ppermute(cot, "space", swap_pairs(count, 1))

    shape = jax.ShapeDtypeStruct
    n_own = FRAMES * PIX
    params = pltpu.CompilerParams(vmem_limit_bytes=32 << 20)
    res, gt, d2, slope1, slope2 = pl.pallas_call(
        forward_kernel,
        out_shape=(
            shape((n_own, C), BF),
            shape((5, C, C), F32),
            shape((n_own, C), BF),
            shape((n_own, C), F32),
            shape((2, n_own, C), F32),
        ),
        scratch_shapes=[
            pltpu.VMEM((5 * FRAMES, LT, C), F32),
            pltpu.VMEM((5 * n_own, C), BF),
        ],
        compiler_params=params,
        cost_estimate=pl.CostEstimate(flops=1 << 30, bytes_accessed=4 << 20, transcendentals=1 << 20),
        name="forward",
    )(base, near, far, cot, conv, up, ws, w_temporal)
    send, keep, low = pl.pallas_call(
        backward_kernel,
        out_shape=(shape((7, C, C), F32), shape((7, C, C), F32), shape((FRAMES * LOW, C), F32)),
        scratch_shapes=[pltpu.VMEM((FRAMES, LT, C), F32)],
        compiler_params=params,
        cost_estimate=pl.CostEstimate(flops=1 << 29, bytes_accessed=4 << 20, transcendentals=0),
        name="backward",
    )(even, odd, d2, slope1, slope2, cot, base, gt, conv_t, up_t, ws, w_temporal)

    low = low.reshape(FRAMES, LROWS, LCOLS, C)
    grad_base = lax.dynamic_slice_in_dim(low, core, 1, 1) + swap_cores(
        lax.dynamic_slice_in_dim(low, 1 - core, 1, 1)
    )
    half = (keep + swap_cores(send)).reshape(7 * C, C)
    half = reduce_chips(half, count, core, at).reshape(7, C, C)
    rest = swap_cores(half)
    grads = jnp.where(
        core == 0, jnp.concatenate([half, rest], axis=0), jnp.concatenate([rest, half], axis=0)
    ).astype(F32)
    return (
        res.reshape(cotangent.shape),
        grad_base,
        grads[:TAPS].reshape(3, 3, C, C),
        grads[TAPS:],
    )


def solution(mesh):
    rows = P(("groups", "space"), "tm", None, None)
    return jax.shard_map(
        local,
        mesh=mesh,
        in_specs=(rows, rows, P(), P()),
        out_specs=(rows, rows, P("groups", None, None, None), P("groups", None, None)),
        check_vma=False,
    )
```

```python
import jax
import jax.numpy as jnp
import numpy as np
from jax import lax
from jax.experimental import pallas as pl
from jax.experimental.pallas import tpu as pltpu
from jax.sharding import PartitionSpec as P

BF = jnp.bfloat16
F32 = jnp.float32
C = 128
FRAMES = 4
ROWS = 4
COLS = 48
LROWS = 2
LCOLS = 12
PIX = ROWS * COLS
LOW = LROWS * LCOLS
TAPS = 9
LT = TAPS * LOW
GROUP = 2 * PIX
BOTH = ("space", "tm")


def up_matrix(n):
    m = np.zeros((4 * n, n))
    for k in range(n):
        lo, hi = max(k - 1, 0), min(k + 1, n - 1)
        for j, (a, at) in enumerate(((0.375, lo), (0.125, lo), (0.125, hi), (0.375, hi))):
            m[4 * k + j, at] += a
            m[4 * k + j, k] += 1.0 - a
    return m


def moved(m, tap):
    out = np.zeros_like(m)
    for i in range(m.shape[0]):
        if 0 <= i + tap - 1 < m.shape[0]:
            out[i] = m[i + tap - 1]
    return out


def constants():
    rows, cols = up_matrix(LROWS), up_matrix(LCOLS)
    up = np.kron(rows, cols).reshape(2, PIX, LOW)
    conv = np.concatenate(
        [np.kron(moved(rows, a), moved(cols, b)) for a in range(3) for b in range(3)], axis=1
    ).reshape(2, PIX, LT)
    as_bf = lambda m: jnp.asarray(m, BF)
    return as_bf(up), as_bf(conv), as_bf(up.transpose(0, 2, 1)), as_bf(conv.transpose(0, 2, 1))


def dot(a, b, dims=((1,), (0,))):
    return lax.dot_general(a, b, (dims, ((), ())), preferred_element_type=F32)


def lanes(parts):
    return jnp.concatenate(parts, axis=1)


def prepare_kernel(
    base, cot_h, conv_h, conv_t_h, up_h, up_t_h, ws_h, wt_h,
    ws, cot, conv, conv_t, time, time_t, big, direct, act, slope1,
    up, up_t, wt, z, sems,
):
    core = lax.axis_index("tm")
    copies = [
        pltpu.make_async_copy(src, dst, sems.at[i])
        for i, (src, dst) in enumerate(
            (
                (ws_h, ws),
                (conv_h.at[core], conv),
                (up_h.at[core], up),
                (cot_h, cot),
                (up_t_h.at[core], up_t),
                (wt_h, wt),
                (conv_t_h.at[core], conv_t),
            )
        )
    ]
    for copy in copies:
        copy.start()
    for copy in copies[:3]:
        copy.wait()
    low_res(base[...], ws, z)
    for p in range(FRAMES // 2):
        pre = dot(conv[...], lanes([z[2 * p], z[2 * p + 1]]).astype(BF))
        sig = jax.nn.sigmoid(pre)
        one = (pre * sig).astype(BF)
        slope = sig * (1.0 + pre * (1.0 - sig))
        for k in range(2):
            lo = p * GROUP + k * PIX
            act[lo : lo + PIX, :] = one[:, k * C : (k + 1) * C]
            slope1[lo : lo + PIX, :] = slope[:, k * C : (k + 1) * C]
    for f in range(FRAMES):
        big[f * PIX : (f + 1) * PIX, :] = dot(up[...], base[f * LOW : (f + 1) * LOW, :]).astype(BF)
    for copy in copies[3:]:
        copy.wait()
    both = dot(up_t[...], lanes([cot[f * PIX : (f + 1) * PIX, :] for f in range(FRAMES)]))
    for f in range(FRAMES):
        direct[f * LOW : (f + 1) * LOW, :] = both[:, f * C : (f + 1) * C]
    zero = jnp.zeros((C, C), BF)
    for k in range(6):
        here = slice(k * C, (k + 1) * C)
        time[here, :C] = wt[k] if k < 5 else zero
        time[here, C:] = wt[k - 1] if k > 0 else zero
        time_t[:C, here] = wt[4 - k] if k < 5 else zero
        time_t[C:, here] = wt[5 - k] if k > 0 else zero


def low_res(block, ws, z):
    frames = block.shape[0] // LOW
    for first in range(0, TAPS, 2):
        taps = range(first, min(first + 2, TAPS))
        prod = dot(block, lanes([ws[tap] for tap in taps]))
        for k, tap in enumerate(taps):
            z[:, tap * LOW : (tap + 1) * LOW, :] = prod[:, k * C : (k + 1) * C].reshape(
                frames, LOW, C
            )


def main_kernel(
    near, far, even, odd, ws, conv, conv_t, act_own, slope1, time, time_t, cot, base,
    send, keep, every, act_near, d2_own, extra, z, act,
):
    core = lax.axis_index("tm")
    at = lax.axis_index("space")
    count = lax.axis_size("space")
    size = FRAMES * LOW
    before = jnp.where(core == 0, near[...], far[...])
    after = jnp.where(core == 0, far[...], near[...])
    none = jnp.zeros((size, C), BF)
    low_res(
        jnp.concatenate(
            [
                jnp.where(at >= 2, before[size:], none),
                jnp.where(at >= 1, before[:size], none),
                jnp.where(at + 1 < count, after[:size], none),
                jnp.where(at + 2 < count, after[size:], none),
            ],
            axis=0,
        ),
        ws,
        z,
    )
    for p in range(2 * FRAMES):
        group = p if p < FRAMES else p + FRAMES // 2
        pre = dot(conv[...], lanes([z[2 * p], z[2 * p + 1]]).astype(BF))
        one = (pre * jax.nn.sigmoid(pre)).astype(BF)
        for k in range(2):
            part = one[:, k * C : (k + 1) * C]
            lo = group * GROUP + k * PIX
            act[lo : lo + PIX, :] = part
            if 2 <= group < 8:
                act_near[lo - 2 * GROUP : lo - 2 * GROUP + PIX, :] = part
    act_near[2 * GROUP : 4 * GROUP, :] = act_own[...]

    def group_of(p):
        if p in (4, 5):
            return act_own[(p - 4) * GROUP : (p - 3) * GROUP, :]
        return act[p * GROUP : (p + 1) * GROUP, :]

    def time_conv(first):
        pre = dot(lanes([group_of(first + k) for k in range(6)]), time[...])
        sig = jax.nn.sigmoid(pre)
        return pre, sig, sig * (1.0 + pre * (1.0 - sig))

    is_even = at % 2 == 0
    blank = jnp.zeros((GROUP, C), BF)
    d2 = []
    for first, inside in ((0, at > 0), (2, None), (4, at < count - 1)):
        pre, sig, slope = time_conv(first)
        for p in range(2):
            here = slice(p * GROUP, (p + 1) * GROUP)
            part = slice(p * C, (p + 1) * C)
            if inside is None:
                got = cot[here, :]
                extra[here, :] = pre[:, part] * sig[:, part]
            else:
                first_choice, other = (odd, even) if first == 0 else (even, odd)
                got = jnp.where(is_even, first_choice[here, :], other[here, :])
                got = jnp.where(inside, got, blank)
            value = (got.astype(F32) * slope[:, part]).astype(BF)
            if inside is None:
                d2_own[here, :] = value
            d2.append(value)

    back = dot(lanes(d2), time_t[...], ((1,), (1,)))
    for p in range(2):
        lo = p * GROUP
        d1 = (back[:, p * C : (p + 1) * C] * slope1[lo : lo + GROUP, :]).astype(BF)
        small = dot(conv_t[...], lanes([d1[:PIX], d1[PIX:]]))
        z[2 * p] = small[:, :C]
        z[2 * p + 1] = small[:, C:]
    every[...] = lanes(
        [
            z[:FRAMES, k * LOW : (k + 1) * LOW, :].reshape(FRAMES * LOW, C).astype(BF)
            for k in range(TAPS)
        ]
    )
    space = dot(base[...], every[...], ((0,), (0,)))
    halve(
        jnp.concatenate([space[:, k * C : (k + 1) * C] for k in range(TAPS)], axis=0),
        core,
        send,
        keep,
    )


def late_kernel(
    act, d2, extra, big, every, ws, direct, res, gt_send, gt_keep, low_send, low_keep
):
    core = lax.axis_index("tm")
    window = lanes([act[k * GROUP : (k + 1) * GROUP, :] for k in range(6)])
    outer = dot(window, lanes([d2[:GROUP, :], d2[GROUP:, :]]), ((0,), (0,)))
    grads = jnp.concatenate(
        [
            outer[t * C : (t + 1) * C, :C] + outer[(t + 1) * C : (t + 2) * C, C:]
            for t in range(5)
        ],
        axis=0,
    )
    halve(grads, core, gt_send, gt_keep)
    total = dot(every[...], lanes([ws[k] for k in range(TAPS)]), ((1,), (1,))) + direct[...]
    for f in range(FRAMES):
        upper = total[f * LOW : f * LOW + LCOLS, :]
        lower = total[f * LOW + LCOLS : (f + 1) * LOW, :]
        low_send[f] = jnp.where(core == 0, lower, upper)
        low_keep[f] = jnp.where(core == 0, upper, lower)
    res[...] = (big[...].astype(F32) + extra[...]).astype(BF)


def halve(grads, core, send, keep):
    rows = grads.shape[0] // 2
    send[...] = jnp.where(core == 0, grads[rows:], grads[:rows]).astype(send.dtype)
    keep[...] = jnp.where(core == 0, grads[:rows], grads[rows:])


def output_kernel(space_half, space_rest, time_half, time_rest, space, time):
    core = lax.axis_index("tm")
    for half, rest, out in ((space_half, space_rest, space), (time_half, time_rest, time)):
        rows = half.shape[0]
        out[:rows] = jnp.where(core == 0, half[...], rest[...]).astype(F32)
        out[rows:] = jnp.where(core == 0, rest[...], half[...]).astype(F32)


def full(pairs, total):
    sources, targets = {a for a, _ in pairs}, {b for _, b in pairs}
    return pairs + list(
        zip(
            [i for i in range(total) if i not in sources],
            [i for i in range(total) if i not in targets],
        )
    )


def hop_pairs(count, hop):
    pairs = []
    for s in range(count):
        pairs.append((2 * s, 2 * (s + hop)) if s + hop < count else (2 * s, 2 * s + 1))
        pairs.append((2 * s + 1, 2 * (s - hop) + 1) if s - hop >= 0 else (2 * s + 1, 2 * s))
    return pairs


def swap_pairs(count, first):
    pairs = []
    for i in range(first, count - 1, 2):
        pairs += [(i, i + 1), (i + 1, i)]
    return full(pairs, count)


def swap_cores(value):
    return lax.ppermute(value, "tm", [(0, 1), (1, 0)])


def reduce_chips(value, count, core, at, levels):
    bits = count.bit_length() - 1
    if count != 1 << bits:
        return lax.psum(value, "space").astype(BF)
    orders = [list(range(bits)), [(b + 2) % bits for b in range(bits)]] if bits > 2 else [list(range(bits))] * 2

    def pairs_of(step):
        pairs = []
        for s in range(count):
            for c in range(2):
                pairs.append((2 * s + c, 2 * (s ^ (1 << orders[c][step])) + c))
        return pairs

    def bit_of(step):
        return jnp.where(core == 0, (at >> orders[0][step]) & 1, (at >> orders[1][step]) & 1)

    levels = min(levels, bits)
    for step in range(levels):
        halves = value.reshape(2, value.shape[0] // 2, C)
        bit = bit_of(step)
        out = lax.dynamic_index_in_dim(halves, 1 - bit, 0, False).astype(BF)
        mine = lax.dynamic_index_in_dim(halves, bit, 0, False)
        value = mine + lax.ppermute(out, BOTH, pairs_of(step)).astype(F32)
    for step in range(levels, bits):
        out = value.astype(BF)
        value = out.astype(F32) + lax.ppermute(out, BOTH, pairs_of(step)).astype(F32)
    value = value.astype(BF)
    for step in reversed(range(levels)):
        got = lax.ppermute(value, BOTH, pairs_of(step))
        value = jnp.where(
            bit_of(step) == 0,
            jnp.concatenate([value, got], axis=0),
            jnp.concatenate([got, value], axis=0),
        )
    return value


def local(base_latent, cotangent, w_spatial, w_temporal):
    core = lax.axis_index("tm")
    at = lax.axis_index("space")
    count = lax.axis_size("space")
    up, conv, up_t, conv_t = constants()
    ws = w_spatial.reshape(TAPS, C, C)
    cot = cotangent.reshape(FRAMES * PIX, C)
    own = base_latent.reshape(FRAMES, LCOLS, C)
    other = swap_cores(own)
    base = jnp.where(
        core == 0, jnp.concatenate([own, other], axis=1), jnp.concatenate([other, own], axis=1)
    ).reshape(FRAMES * LOW, C)
    even, odd = (lax.ppermute(cot, "space", swap_pairs(count, first)) for first in (0, 1))
    near = jnp.concatenate(
        [lax.ppermute(base, BOTH, hop_pairs(count, hop)) for hop in (1, 2)], axis=0
    )

    shape = jax.ShapeDtypeStruct
    n_own = FRAMES * PIX
    params = pltpu.CompilerParams(vmem_limit_bytes=32 << 20)
    vmem = pl.BlockSpec(memory_space=pltpu.VMEM)
    hbm = pl.BlockSpec(memory_space=pltpu.HBM)
    cost = lambda flops: pl.CostEstimate(flops=flops, bytes_accessed=2 << 20, transcendentals=0)
    ws_v, cot_v, conv_v, conv_t_v, time, time_t, big, direct, act, slope1 = pl.pallas_call(
        prepare_kernel,
        in_specs=[vmem] + [hbm] * 7,
        out_shape=(
            shape((TAPS, C, C), BF),
            shape((n_own, C), BF),
            shape((PIX, LT), BF),
            shape((LT, PIX), BF),
            shape((6 * C, 2 * C), BF),
            shape((2 * C, 6 * C), BF),
            shape((n_own, C), BF),
            shape((FRAMES * LOW, C), F32),
            shape((n_own, C), BF),
            shape((n_own, C), F32),
        ),
        scratch_shapes=[
            pltpu.VMEM((PIX, LOW), BF),
            pltpu.VMEM((LOW, PIX), BF),
            pltpu.VMEM((5, C, C), BF),
            pltpu.VMEM((FRAMES, LT, C), F32),
            pltpu.SemaphoreType.DMA((7,)),
        ],
        compiler_params=params,
        cost_estimate=cost(1 << 29),
        name="prepare",
    )(base, *(pltpu.with_memory_space_constraint(x, pltpu.HBM) for x in (cot, conv, conv_t, up, up_t, ws, w_temporal)))
    near, even, cot_v = lax.optimization_barrier((near, even, cot_v))
    far = swap_cores(near)
    half_space = TAPS * C // 2
    half_time = 5 * C // 2
    send, keep, every, act_near, d2, extra = pl.pallas_call(
        main_kernel,
        out_shape=(
            shape((half_space, C), BF),
            shape((half_space, C), F32),
            shape((FRAMES * LOW, TAPS * C), BF),
            shape((6 * GROUP, C), BF),
            shape((n_own, C), BF),
            shape((n_own, C), F32),
        ),
        scratch_shapes=[
            pltpu.VMEM((4 * FRAMES, LT, C), F32),
            pltpu.VMEM((5 * n_own, C), BF),
        ],
        compiler_params=params,
        cost_estimate=cost(1 << 30),
        name="main",
    )(near, far, even, odd, ws_v, conv_v, conv_t_v, act, slope1, time, time_t, cot_v, base)
    res, gt_send, gt_keep, low_send, low_keep = pl.pallas_call(
        late_kernel,
        out_shape=(
            shape((n_own, C), BF),
            shape((half_time, C), BF),
            shape((half_time, C), F32),
            shape((FRAMES, LCOLS, C), F32),
            shape((FRAMES, LCOLS, C), F32),
        ),
        compiler_params=params,
        cost_estimate=cost(1 << 29),
        name="late",
    )(act_near, d2, extra, big, every, ws_v, direct)

    grad_base = low_keep + swap_cores(low_send)
    halves = []
    for out, mine, levels in ((gt_send, gt_keep, 0), (send, keep, 1)):
        halves.append(reduce_chips(mine + swap_cores(out).astype(F32), count, core, at, levels))
    time_half, space_half = halves
    grad_spatial, grad_temporal = pl.pallas_call(
        output_kernel,
        out_shape=(shape((TAPS * C, C), F32), shape((5 * C, C), F32)),
        compiler_params=params,
        name="output",
    )(space_half, swap_cores(space_half), time_half, swap_cores(time_half))
    return (
        res.reshape(cotangent.shape),
        grad_base.reshape(base_latent.shape),
        grad_spatial.reshape(3, 3, C, C),
        grad_temporal.reshape(5, C, C),
    )


def solution(mesh):
    rows = P(("groups", "space"), "tm", None, None)
    return jax.shard_map(
        local,
        mesh=mesh,
        in_specs=(rows, rows, P(), P()),
        out_specs=(rows, rows, P("groups", None, None, None), P("groups", None, None)),
        check_vma=False,
    )
```

```python
import jax
import jax.numpy as jnp
import numpy as np
from jax import lax
from jax.experimental import pallas as pl
from jax.experimental.pallas import tpu as pltpu
from jax.sharding import PartitionSpec as P

BF = jnp.bfloat16
F32 = jnp.float32
C = 128
FRAMES = 4
ROWS = 4
COLS = 48
LROWS = 2
LCOLS = 12
PIX = ROWS * COLS
LOW = LROWS * LCOLS
TAPS = 9
LT = TAPS * LOW
GROUP = 2 * PIX
BOTH = ("space", "tm")
EXT = ROWS + 2
WIDE = 3 * EXT * COLS
DEEP = 12 * C


def up_matrix(n):
    m = np.zeros((4 * n, n))
    for k in range(n):
        lo, hi = max(k - 1, 0), min(k + 1, n - 1)
        for j, (a, at) in enumerate(((0.375, lo), (0.125, lo), (0.125, hi), (0.375, hi))):
            m[4 * k + j, at] += a
            m[4 * k + j, k] += 1.0 - a
    return m


def moved(m, tap):
    out = np.zeros_like(m)
    for i in range(m.shape[0]):
        if 0 <= i + tap - 1 < m.shape[0]:
            out[i] = m[i + tap - 1]
    return out


def constants():
    rows, cols = up_matrix(LROWS), up_matrix(LCOLS)
    tall = np.pad(rows, ((1, 1), (0, 0)))
    wide = np.stack(
        [
            np.concatenate(
                [np.kron(tall[core * ROWS : core * ROWS + EXT], moved(cols, b)) for b in range(3)]
            )
            for core in range(2)
        ]
    )
    up = np.kron(rows, cols).reshape(2, PIX, LOW)
    conv = np.concatenate(
        [np.kron(moved(rows, a), moved(cols, b)) for a in range(3) for b in range(3)], axis=1
    ).reshape(2, PIX, LT)
    as_bf = lambda m: jnp.asarray(m, BF)
    return as_bf(wide), as_bf(up.transpose(0, 2, 1)), as_bf(conv.transpose(0, 2, 1))


def dot(a, b, dims=((1,), (0,))):
    return lax.dot_general(a, b, (dims, ((), ())), preferred_element_type=F32)


def lanes(parts):
    return jnp.concatenate(parts, axis=1)


def prepare_kernel(
    base, cot_h, wide_h, conv_t_h, up_t_h, ws_h, wt_h,
    ws, cot, wide, conv_t, deep, time, time_t, big, direct, act, slope1,
    up_t, wt, u3, lhs, sems,
):
    core = lax.axis_index("tm")
    copies = [
        pltpu.make_async_copy(src, dst, sems.at[i])
        for i, (src, dst) in enumerate(
            (
                (ws_h, ws),
                (wide_h.at[core], wide),
                (cot_h, cot),
                (up_t_h.at[core], up_t),
                (wt_h, wt),
                (conv_t_h.at[core], conv_t),
            )
        )
    ]
    for copy in copies:
        copy.start()
    for copy in copies[:2]:
        copy.wait()
    zero = jnp.zeros((C, C), BF)
    for b in range(3):
        for d in range(4):
            here = slice((b * 4 + d) * C, (b * 4 + d + 1) * C)
            deep[here, :C] = ws[3 * d + b] if d < 3 else zero
            deep[here, C:] = ws[3 * (d - 1) + b] if d > 0 else zero
    frames = [base[f * LOW : (f + 1) * LOW, :] for f in range(FRAMES)]
    pre = conv_space(frames, wide, deep, u3, lhs)[0]
    sig = jax.nn.sigmoid(pre)
    one = (pre * sig).astype(BF)
    slope = sig * (1.0 + pre * (1.0 - sig))
    for f in range(FRAMES):
        here = slice(f * PIX, (f + 1) * PIX)
        act[here, :] = image_order(one, f)
        slope1[here, :] = image_order(slope, f)
        big[here, :] = u3[f, (EXT + 1) * COLS : (EXT + 1) * COLS + PIX, :]
    for copy in copies[2:]:
        copy.wait()
    both = dot(up_t[...], lanes([cot[f * PIX : (f + 1) * PIX, :] for f in range(FRAMES)]))
    for f in range(FRAMES):
        direct[f * LOW : (f + 1) * LOW, :] = both[:, f * C : (f + 1) * C]
    for k in range(6):
        here = slice(k * C, (k + 1) * C)
        time[here, :C] = wt[k] if k < 5 else zero
        time[here, C:] = wt[k - 1] if k > 0 else zero
        time_t[:C, here] = wt[4 - k] if k < 5 else zero
        time_t[C:, here] = wt[5 - k] if k > 0 else zero


def conv_space(base_rows, wide, weights, u3, lhs):
    count = len(base_rows)
    for f in range(0, count, 2):
        both = dot(wide[...], lanes(base_rows[f : f + 2])).astype(BF)
        u3[f] = both[:, :C]
        u3[f + 1] = both[:, C:]
    for f in range(count):
        for q in range(2):
            to = (2 * f + q) * COLS
            for b in range(3):
                for d in range(4):
                    frm = (b * EXT + 2 * q + d) * COLS
                    block = b * 4 + d
                    lhs[to : to + COLS, block * C : (block + 1) * C] = u3[f, frm : frm + COLS, :]
    rows = count * PIX // 2
    return [
        dot(lhs[first : first + 2 * PIX, :], weights[...]) for first in range(0, rows, 2 * PIX)
    ]


def image_order(pairs, f):
    out = []
    for q in range(2):
        here = slice((2 * f + q) * COLS, (2 * f + q + 1) * COLS)
        out += [pairs[here, :C], pairs[here, C:]]
    return jnp.concatenate(out, axis=0)


def main_kernel(
    near, far, even, odd, wide, deep, conv_t, act_own, slope1, time, time_t, cot, base,
    send, keep, every, act_near, d2_own, extra, z, act, u3, lhs,
):
    core = lax.axis_index("tm")
    at = lax.axis_index("space")
    count = lax.axis_size("space")
    size = FRAMES * LOW
    before = jnp.where(core == 0, near[...], far[...])
    after = jnp.where(core == 0, far[...], near[...])
    none = jnp.zeros((size, C), BF)
    blocks = (
        jnp.where(at >= 2, before[size:], none),
        jnp.where(at >= 1, before[:size], none),
        jnp.where(at + 1 < count, after[:size], none),
        jnp.where(at + 2 < count, after[size:], none),
    )
    frames = [block[f * LOW : (f + 1) * LOW] for block in blocks for f in range(FRAMES)]
    for k, pre in enumerate(conv_space(frames, wide, deep, u3, lhs)):
        one = (pre * jax.nn.sigmoid(pre)).astype(BF)
        for f in range(FRAMES):
            part = image_order(one, f)
            lo = (FRAMES * (k if k < 2 else k + 1) + f) * PIX
            act[lo : lo + PIX, :] = part
            if 2 * GROUP <= lo < 8 * GROUP:
                act_near[lo - 2 * GROUP : lo - 2 * GROUP + PIX, :] = part
    act_near[2 * GROUP : 4 * GROUP, :] = act_own[...]

    def group_of(p):
        if p in (4, 5):
            return act_own[(p - 4) * GROUP : (p - 3) * GROUP, :]
        return act[p * GROUP : (p + 1) * GROUP, :]

    def time_conv(first):
        pre = dot(lanes([group_of(first + k) for k in range(6)]), time[...])
        sig = jax.nn.sigmoid(pre)
        return pre, sig, sig * (1.0 + pre * (1.0 - sig))

    is_even = at % 2 == 0
    blank = jnp.zeros((GROUP, C), BF)
    d2 = []
    for first, inside in ((0, at > 0), (2, None), (4, at < count - 1)):
        pre, sig, slope = time_conv(first)
        for p in range(2):
            here = slice(p * GROUP, (p + 1) * GROUP)
            part = slice(p * C, (p + 1) * C)
            if inside is None:
                got = cot[here, :]
                extra[here, :] = pre[:, part] * sig[:, part]
            else:
                first_choice, other = (odd, even) if first == 0 else (even, odd)
                got = jnp.where(is_even, first_choice[here, :], other[here, :])
                got = jnp.where(inside, got, blank)
            value = (got.astype(F32) * slope[:, part]).astype(BF)
            if inside is None:
                d2_own[here, :] = value
            d2.append(value)

    back = dot(lanes(d2), time_t[...], ((1,), (1,)))
    for p in range(2):
        lo = p * GROUP
        d1 = (back[:, p * C : (p + 1) * C] * slope1[lo : lo + GROUP, :]).astype(BF)
        small = dot(conv_t[...], lanes([d1[:PIX], d1[PIX:]]))
        z[2 * p] = small[:, :C]
        z[2 * p + 1] = small[:, C:]
    every[...] = lanes(
        [
            z[:FRAMES, k * LOW : (k + 1) * LOW, :].reshape(FRAMES * LOW, C).astype(BF)
            for k in range(TAPS)
        ]
    )
    space = dot(base[...], every[...], ((0,), (0,)))
    halve(
        jnp.concatenate([space[:, k * C : (k + 1) * C] for k in range(TAPS)], axis=0),
        core,
        send,
        keep,
    )


def late_kernel(
    act, d2, extra, big, every, ws, direct, res, gt_send, gt_keep, low_send, low_keep
):
    core = lax.axis_index("tm")
    window = lanes([act[k * GROUP : (k + 1) * GROUP, :] for k in range(6)])
    outer = dot(window, lanes([d2[:GROUP, :], d2[GROUP:, :]]), ((0,), (0,)))
    grads = jnp.concatenate(
        [
            outer[t * C : (t + 1) * C, :C] + outer[(t + 1) * C : (t + 2) * C, C:]
            for t in range(5)
        ],
        axis=0,
    )
    halve(grads, core, gt_send, gt_keep)
    total = dot(every[...], lanes([ws[k] for k in range(TAPS)]), ((1,), (1,))) + direct[...]
    for f in range(FRAMES):
        upper = total[f * LOW : f * LOW + LCOLS, :]
        lower = total[f * LOW + LCOLS : (f + 1) * LOW, :]
        low_send[f] = jnp.where(core == 0, lower, upper)
        low_keep[f] = jnp.where(core == 0, upper, lower)
    res[...] = (big[...].astype(F32) + extra[...]).astype(BF)


def halve(grads, core, send, keep):
    rows = grads.shape[0] // 2
    send[...] = jnp.where(core == 0, grads[rows:], grads[:rows]).astype(send.dtype)
    keep[...] = jnp.where(core == 0, grads[:rows], grads[rows:])


def output_kernel(space_half, space_rest, time_half, time_rest, space, time):
    core = lax.axis_index("tm")
    for half, rest, out in ((space_half, space_rest, space), (time_half, time_rest, time)):
        rows = half.shape[0]
        out[:rows] = jnp.where(core == 0, half[...], rest[...]).astype(F32)
        out[rows:] = jnp.where(core == 0, rest[...], half[...]).astype(F32)


def full(pairs, total):
    sources, targets = {a for a, _ in pairs}, {b for _, b in pairs}
    return pairs + list(
        zip(
            [i for i in range(total) if i not in sources],
            [i for i in range(total) if i not in targets],
        )
    )


def hop_pairs(count, hop):
    pairs = []
    for s in range(count):
        pairs.append((2 * s, 2 * (s + hop)) if s + hop < count else (2 * s, 2 * s + 1))
        pairs.append((2 * s + 1, 2 * (s - hop) + 1) if s - hop >= 0 else (2 * s + 1, 2 * s))
    return pairs


def swap_pairs(count, first):
    pairs = []
    for i in range(first, count - 1, 2):
        pairs += [(i, i + 1), (i + 1, i)]
    return full(pairs, count)


def swap_cores(value):
    return lax.ppermute(value, "tm", [(0, 1), (1, 0)])


def reduce_chips(value, count, core, at, levels):
    bits = count.bit_length() - 1
    if count != 1 << bits:
        return lax.psum(value, "space").astype(BF)
    plain = list(range(bits))
    orders = [plain, plain[1::-1] + plain[2:] if levels else plain[-1:] + plain[:-1]]

    def pairs_of(step):
        pairs = []
        for s in range(count):
            for c in range(2):
                pairs.append((2 * s + c, 2 * (s ^ (1 << orders[c][step])) + c))
        return pairs

    def bit_of(step):
        return jnp.where(core == 0, (at >> orders[0][step]) & 1, (at >> orders[1][step]) & 1)

    levels = min(levels, bits)
    for step in range(levels):
        halves = value.reshape(2, value.shape[0] // 2, C)
        bit = bit_of(step)
        out = lax.dynamic_index_in_dim(halves, 1 - bit, 0, False).astype(BF)
        mine = lax.dynamic_index_in_dim(halves, bit, 0, False)
        value = mine + lax.ppermute(out, BOTH, pairs_of(step)).astype(F32)
    for step in range(levels, bits):
        out = value.astype(BF)
        value = out.astype(F32) + lax.ppermute(out, BOTH, pairs_of(step)).astype(F32)
    value = value.astype(BF)
    for step in reversed(range(levels)):
        got = lax.ppermute(value, BOTH, pairs_of(step))
        value = jnp.where(
            bit_of(step) == 0,
            jnp.concatenate([value, got], axis=0),
            jnp.concatenate([got, value], axis=0),
        )
    return value


def local(base_latent, cotangent, w_spatial, w_temporal):
    core = lax.axis_index("tm")
    at = lax.axis_index("space")
    count = lax.axis_size("space")
    wide, up_t, conv_t = constants()
    ws = w_spatial.reshape(TAPS, C, C)
    cot = cotangent.reshape(FRAMES * PIX, C)
    own = base_latent.reshape(FRAMES, LCOLS, C)
    other = swap_cores(own)
    base = jnp.where(
        core == 0, jnp.concatenate([own, other], axis=1), jnp.concatenate([other, own], axis=1)
    ).reshape(FRAMES * LOW, C)
    even, odd = (lax.ppermute(cot, "space", swap_pairs(count, first)) for first in (0, 1))
    near = jnp.concatenate(
        [lax.ppermute(base, BOTH, hop_pairs(count, hop)) for hop in (1, 2)], axis=0
    )

    shape = jax.ShapeDtypeStruct
    n_own = FRAMES * PIX
    params = pltpu.CompilerParams(vmem_limit_bytes=32 << 20)
    vmem = pl.BlockSpec(memory_space=pltpu.VMEM)
    hbm = pl.BlockSpec(memory_space=pltpu.HBM)
    cost = lambda flops: pl.CostEstimate(flops=flops, bytes_accessed=2 << 20, transcendentals=0)
    ws_v, cot_v, wide_v, conv_t_v, deep, time, time_t, big, direct, act, slope1 = pl.pallas_call(
        prepare_kernel,
        in_specs=[vmem] + [hbm] * 6,
        out_shape=(
            shape((TAPS, C, C), BF),
            shape((n_own, C), BF),
            shape((WIDE, LOW), BF),
            shape((LT, PIX), BF),
            shape((DEEP, 2 * C), BF),
            shape((6 * C, 2 * C), BF),
            shape((2 * C, 6 * C), BF),
            shape((n_own, C), BF),
            shape((FRAMES * LOW, C), F32),
            shape((n_own, C), BF),
            shape((n_own, C), F32),
        ),
        scratch_shapes=[
            pltpu.VMEM((LOW, PIX), BF),
            pltpu.VMEM((5, C, C), BF),
            pltpu.VMEM((FRAMES, WIDE, C), BF),
            pltpu.VMEM((FRAMES * PIX // 2, DEEP), BF),
            pltpu.SemaphoreType.DMA((6,)),
        ],
        compiler_params=params,
        cost_estimate=cost(1 << 29),
        name="prepare",
    )(base, *(pltpu.with_memory_space_constraint(x, pltpu.HBM) for x in (cot, wide, conv_t, up_t, ws, w_temporal)))
    near, even, cot_v = lax.optimization_barrier((near, even, cot_v))
    far = swap_cores(near)
    half_space = TAPS * C // 2
    half_time = 5 * C // 2
    send, keep, every, act_near, d2, extra = pl.pallas_call(
        main_kernel,
        out_shape=(
            shape((half_space, C), BF),
            shape((half_space, C), F32),
            shape((FRAMES * LOW, TAPS * C), BF),
            shape((6 * GROUP, C), BF),
            shape((n_own, C), BF),
            shape((n_own, C), F32),
        ),
        scratch_shapes=[
            pltpu.VMEM((FRAMES, LT, C), F32),
            pltpu.VMEM((5 * n_own, C), BF),
            pltpu.VMEM((4 * FRAMES, WIDE, C), BF),
            pltpu.VMEM((4 * FRAMES * PIX // 2, DEEP), BF),
        ],
        compiler_params=params,
        cost_estimate=cost(1 << 30),
        name="main",
    )(near, far, even, odd, wide_v, deep, conv_t_v, act, slope1, time, time_t, cot_v, base)
    res, gt_send, gt_keep, low_send, low_keep = pl.pallas_call(
        late_kernel,
        out_shape=(
            shape((n_own, C), BF),
            shape((half_time, C), BF),
            shape((half_time, C), F32),
            shape((FRAMES, LCOLS, C), F32),
            shape((FRAMES, LCOLS, C), F32),
        ),
        compiler_params=params,
        cost_estimate=cost(1 << 29),
        name="late",
    )(act_near, d2, extra, big, every, ws_v, direct)

    grad_base = low_keep + swap_cores(low_send)
    halves = []
    for out, mine, levels in ((gt_send, gt_keep, 0), (send, keep, 1)):
        halves.append(reduce_chips(mine + swap_cores(out).astype(F32), count, core, at, levels))
    time_half, space_half = halves
    grad_spatial, grad_temporal = pl.pallas_call(
        output_kernel,
        out_shape=(shape((TAPS * C, C), F32), shape((5 * C, C), F32)),
        compiler_params=params,
        name="output",
    )(space_half, swap_cores(space_half), time_half, swap_cores(time_half))
    return (
        res.reshape(cotangent.shape),
        grad_base.reshape(base_latent.shape),
        grad_spatial.reshape(3, 3, C, C),
        grad_temporal.reshape(5, C, C),
    )


def solution(mesh):
    rows = P(("groups", "space"), "tm", None, None)
    return jax.shard_map(
        local,
        mesh=mesh,
        in_specs=(rows, rows, P(), P()),
        out_specs=(rows, rows, P("groups", None, None, None), P("groups", None, None)),
        check_vma=False,
    )
```

```python
import jax
import jax.numpy as jnp
import numpy as np
from jax import lax
from jax.experimental import pallas as pl
from jax.experimental.pallas import tpu as pltpu
from jax.sharding import PartitionSpec as P

BF = jnp.bfloat16
F32 = jnp.float32
C = 128
FRAMES = 4
ROWS = 4
COLS = 48
LROWS = 2
LCOLS = 12
PIX = ROWS * COLS
LOW = LROWS * LCOLS
TAPS = 9
LT = TAPS * LOW
GROUP = 2 * PIX
BOTH = ("space", "tm")
EXT = ROWS + 2
WIDE = 3 * EXT * COLS
DEEP = 12 * C


def up_matrix(n):
    m = np.zeros((4 * n, n))
    for k in range(n):
        lo, hi = max(k - 1, 0), min(k + 1, n - 1)
        for j, (a, at) in enumerate(((0.375, lo), (0.125, lo), (0.125, hi), (0.375, hi))):
            m[4 * k + j, at] += a
            m[4 * k + j, k] += 1.0 - a
    return m


def moved(m, tap):
    out = np.zeros_like(m)
    for i in range(m.shape[0]):
        if 0 <= i + tap - 1 < m.shape[0]:
            out[i] = m[i + tap - 1]
    return out


def constants():
    rows, cols = up_matrix(LROWS), up_matrix(LCOLS)
    tall = np.pad(rows, ((1, 1), (0, 0)))
    wide = np.stack(
        [
            np.concatenate(
                [np.kron(tall[core * ROWS : core * ROWS + EXT], moved(cols, b)) for b in range(3)]
            )
            for core in range(2)
        ]
    )
    up = np.kron(rows, cols).reshape(2, PIX, LOW)
    conv = np.concatenate(
        [np.kron(moved(rows, a), moved(cols, b)) for a in range(3) for b in range(3)], axis=1
    ).reshape(2, PIX, LT)
    as_bf = lambda m: jnp.asarray(m, BF)
    return as_bf(wide), as_bf(up.transpose(0, 2, 1)), as_bf(conv.transpose(0, 2, 1))


def dot(a, b, dims=((1,), (0,))):
    return lax.dot_general(a, b, (dims, ((), ())), preferred_element_type=F32)


def lanes(parts):
    return jnp.concatenate(parts, axis=1)


def weights_kernel(
    cot_h, wide_h, conv_t_h, up_t_h, ws_h, wt_h, ws, cot, wide, conv_t, up_t, deep, time, time_t, wt, sems
):
    core = lax.axis_index("tm")
    copies = [
        pltpu.make_async_copy(src, dst, sems.at[i])
        for i, (src, dst) in enumerate(
            (
                (ws_h, ws),
                (wt_h, wt),
                (cot_h, cot),
                (wide_h.at[core], wide),
                (up_t_h.at[core], up_t),
                (conv_t_h.at[core], conv_t),
            )
        )
    ]
    for copy in copies:
        copy.start()
    for copy in copies:
        copy.wait()
    zero = jnp.zeros((C, C), BF)
    for b in range(3):
        for d in range(4):
            here = slice((b * 4 + d) * C, (b * 4 + d + 1) * C)
            deep[here, :C] = ws[3 * d + b] if d < 3 else zero
            deep[here, C:] = ws[3 * (d - 1) + b] if d > 0 else zero
    for k in range(6):
        here = slice(k * C, (k + 1) * C)
        time[here, :C] = wt[k] if k < 5 else zero
        time[here, C:] = wt[k - 1] if k > 0 else zero
        time_t[:C, here] = wt[4 - k] if k < 5 else zero
        time_t[C:, here] = wt[5 - k] if k > 0 else zero


def prepare_kernel(base, wide, deep, up_t, cot, big, direct, act, slope1, u3, lhs):
    frames = [base[f * LOW : (f + 1) * LOW, :] for f in range(FRAMES)]
    pre = conv_space(frames, wide, deep, u3, lhs)[0]
    sig = jax.nn.sigmoid(pre)
    one = (pre * sig).astype(BF)
    slope = sig * (1.0 + pre * (1.0 - sig))
    for f in range(FRAMES):
        here = slice(f * PIX, (f + 1) * PIX)
        act[here, :] = image_order(one, f)
        slope1[here, :] = image_order(slope, f)
        big[here, :] = u3[f, (EXT + 1) * COLS : (EXT + 1) * COLS + PIX, :]
    both = dot(up_t[...], lanes([cot[f * PIX : (f + 1) * PIX, :] for f in range(FRAMES)]))
    for f in range(FRAMES):
        direct[f * LOW : (f + 1) * LOW, :] = both[:, f * C : (f + 1) * C]


def conv_space(base_rows, wide, weights, u3, lhs):
    count = len(base_rows)
    for f in range(0, count, 2):
        both = dot(wide[...], lanes(base_rows[f : f + 2])).astype(BF)
        u3[f] = both[:, :C]
        u3[f + 1] = both[:, C:]
    for f in range(count):
        for q in range(2):
            to = (2 * f + q) * COLS
            for b in range(3):
                for d in range(4):
                    frm = (b * EXT + 2 * q + d) * COLS
                    block = b * 4 + d
                    lhs[to : to + COLS, block * C : (block + 1) * C] = u3[f, frm : frm + COLS, :]
    rows = count * PIX // 2
    return [
        dot(lhs[first : first + 2 * PIX, :], weights[...]) for first in range(0, rows, 2 * PIX)
    ]


def image_order(pairs, f):
    out = []
    for q in range(2):
        here = slice((2 * f + q) * COLS, (2 * f + q + 1) * COLS)
        out += [pairs[here, :C], pairs[here, C:]]
    return jnp.concatenate(out, axis=0)


def forward_kernel(
    near, far, wide, deep, act_own, time, cot, big, res, gt_send, gt_keep, d2, slope2, act, u3, lhs
):
    core = lax.axis_index("tm")
    at = lax.axis_index("space")
    count = lax.axis_size("space")
    size = FRAMES * LOW
    before = jnp.where(core == 0, near[...], far[...])
    after = jnp.where(core == 0, far[...], near[...])
    none = jnp.zeros((size, C), BF)
    blocks = (
        jnp.where(at >= 2, before[size:], none),
        jnp.where(at >= 1, before[:size], none),
        jnp.where(at + 1 < count, after[:size], none),
        jnp.where(at + 2 < count, after[size:], none),
    )
    frames = [block[f * LOW : (f + 1) * LOW] for block in blocks for f in range(FRAMES)]
    for k, pre in enumerate(conv_space(frames, wide, deep, u3, lhs)):
        one = (pre * jax.nn.sigmoid(pre)).astype(BF)
        for f in range(FRAMES):
            lo = (FRAMES * (k if k < 2 else k + 1) + f) * PIX
            act[lo : lo + PIX, :] = image_order(one, f)

    def group_of(p):
        if p in (4, 5):
            return act_own[(p - 4) * GROUP : (p - 3) * GROUP, :]
        return act[p * GROUP : (p + 1) * GROUP, :]

    def window(first):
        return lanes([group_of(first + k) for k in range(6)])

    def time_conv(first):
        pre = dot(window(first), time[...])
        sig = jax.nn.sigmoid(pre)
        return pre, sig, sig * (1.0 + pre * (1.0 - sig))

    pre, sig, slope = time_conv(2)
    extra = pre * sig
    for p in range(2):
        here = slice(p * GROUP, (p + 1) * GROUP)
        part = slice(p * C, (p + 1) * C)
        res[here, :] = (big[here, :].astype(F32) + extra[:, part]).astype(BF)
        d2[here, :] = (cot[here, :].astype(F32) * slope[:, part]).astype(BF)
    for side, first in ((0, 0), (1, 4)):
        slope = time_conv(first)[2]
        for p in range(2):
            slope2[side, p * GROUP : (p + 1) * GROUP, :] = slope[:, p * C : (p + 1) * C]

    outer = dot(window(2), lanes([d2[:GROUP, :], d2[GROUP:, :]]), ((0,), (0,)))
    grads = jnp.concatenate(
        [
            outer[t * C : (t + 1) * C, :C] + outer[(t + 1) * C : (t + 2) * C, C:]
            for t in range(5)
        ],
        axis=0,
    )
    halve(grads, core, gt_send, gt_keep)


def halve(grads, core, send, keep):
    rows = grads.shape[0] // 2
    send[...] = jnp.where(core == 0, grads[rows:], grads[:rows]).astype(send.dtype)
    keep[...] = jnp.where(core == 0, grads[:rows], grads[rows:])


def backward_kernel(
    even, odd, d2, slope1, slope2, base, conv_t, time_t, send, keep, every, dsc,
):
    core = lax.axis_index("tm")
    at = lax.axis_index("space")
    count = lax.axis_size("space")
    is_even = at % 2 == 0
    zeros = jnp.zeros((FRAMES * PIX, C), F32)

    def outside(first, second, inside, side):
        got = jnp.where(is_even, first[...], second[...]).astype(F32)
        return jnp.where(inside, got * slope2[side], zeros).astype(BF)

    before = outside(odd, even, at > 0, 0)
    after = outside(even, odd, at < count - 1, 1)
    window = lanes(
        [before[:GROUP], before[GROUP:], d2[:GROUP, :], d2[GROUP:, :], after[:GROUP], after[GROUP:]]
    )
    back = dot(window, time_t[...], ((1,), (1,)))
    for p in range(2):
        lo = p * GROUP
        d1 = (back[:, p * C : (p + 1) * C] * slope1[lo : lo + GROUP, :]).astype(BF)
        small = dot(conv_t[...], lanes([d1[:PIX], d1[PIX:]]))
        dsc[2 * p] = small[:, :C]
        dsc[2 * p + 1] = small[:, C:]
    every[...] = lanes(
        [dsc[:, k * LOW : (k + 1) * LOW, :].reshape(FRAMES * LOW, C).astype(BF) for k in range(TAPS)]
    )
    space = dot(base[...], every[...], ((0,), (0,)))
    halve(
        jnp.concatenate([space[:, k * C : (k + 1) * C] for k in range(TAPS)], axis=0),
        core,
        send,
        keep,
    )


def late_kernel(every, ws, direct, low_send, low_keep):
    core = lax.axis_index("tm")
    total = dot(every[...], lanes([ws[k] for k in range(TAPS)]), ((1,), (1,))) + direct[...]
    for f in range(FRAMES):
        upper = total[f * LOW : f * LOW + LCOLS, :]
        lower = total[f * LOW + LCOLS : (f + 1) * LOW, :]
        low_send[f] = jnp.where(core == 0, lower, upper)
        low_keep[f] = jnp.where(core == 0, upper, lower)


def output_kernel(space_half, space_rest, time_half, time_rest, space, time):
    core = lax.axis_index("tm")
    for half, rest, out in ((space_half, space_rest, space), (time_half, time_rest, time)):
        rows = half.shape[0]
        out[:rows] = jnp.where(core == 0, half[...], rest[...]).astype(F32)
        out[rows:] = jnp.where(core == 0, rest[...], half[...]).astype(F32)


def full(pairs, total):
    sources, targets = {a for a, _ in pairs}, {b for _, b in pairs}
    return pairs + list(
        zip(
            [i for i in range(total) if i not in sources],
            [i for i in range(total) if i not in targets],
        )
    )


def hop_pairs(count, hop):
    pairs = []
    for s in range(count):
        pairs.append((2 * s, 2 * (s + hop)) if s + hop < count else (2 * s, 2 * s + 1))
        pairs.append((2 * s + 1, 2 * (s - hop) + 1) if s - hop >= 0 else (2 * s + 1, 2 * s))
    return pairs


def swap_pairs(count, first):
    pairs = []
    for i in range(first, count - 1, 2):
        pairs += [(i, i + 1), (i + 1, i)]
    return full(pairs, count)


def swap_cores(value):
    return lax.ppermute(value, "tm", [(0, 1), (1, 0)])


def reduce_chips(value, count, core, at, levels):
    bits = count.bit_length() - 1
    if count != 1 << bits:
        return lax.psum(value, "space").astype(BF)
    plain = list(range(bits))
    orders = [plain, plain[1::-1] + plain[2:] if levels else plain[-1:] + plain[:-1]]

    def pairs_of(step):
        pairs = []
        for s in range(count):
            for c in range(2):
                pairs.append((2 * s + c, 2 * (s ^ (1 << orders[c][step])) + c))
        return pairs

    def bit_of(step):
        return jnp.where(core == 0, (at >> orders[0][step]) & 1, (at >> orders[1][step]) & 1)

    levels = min(levels, bits)
    for step in range(levels):
        halves = value.reshape(2, value.shape[0] // 2, C)
        bit = bit_of(step)
        out = lax.dynamic_index_in_dim(halves, 1 - bit, 0, False).astype(BF)
        mine = lax.dynamic_index_in_dim(halves, bit, 0, False)
        value = mine + lax.ppermute(out, BOTH, pairs_of(step)).astype(F32)
    for step in range(levels, bits):
        out = value.astype(BF)
        value = out.astype(F32) + lax.ppermute(out, BOTH, pairs_of(step)).astype(F32)
    value = value.astype(BF)
    for step in reversed(range(levels)):
        got = lax.ppermute(value, BOTH, pairs_of(step))
        value = jnp.where(
            bit_of(step) == 0,
            jnp.concatenate([value, got], axis=0),
            jnp.concatenate([got, value], axis=0),
        )
    return value


def local(base_latent, cotangent, w_spatial, w_temporal):
    core = lax.axis_index("tm")
    at = lax.axis_index("space")
    count = lax.axis_size("space")
    wide, up_t, conv_t = constants()
    ws = w_spatial.reshape(TAPS, C, C)
    cot = cotangent.reshape(FRAMES * PIX, C)
    own = base_latent.reshape(FRAMES, LCOLS, C)
    shape = jax.ShapeDtypeStruct
    n_own = FRAMES * PIX
    params = pltpu.CompilerParams(vmem_limit_bytes=32 << 20)
    vmem = pl.BlockSpec(memory_space=pltpu.VMEM)
    hbm = pl.BlockSpec(memory_space=pltpu.HBM)
    cost = lambda flops: pl.CostEstimate(flops=flops, bytes_accessed=2 << 20, transcendentals=0)
    ws_v, cot_v, wide_v, conv_t_v, up_t_v, deep, time, time_t = pl.pallas_call(
        weights_kernel,
        in_specs=[pl.BlockSpec(memory_space=pltpu.HBM)] * 6,
        out_shape=(
            shape((TAPS, C, C), BF),
            shape((n_own, C), BF),
            shape((WIDE, LOW), BF),
            shape((LT, PIX), BF),
            shape((LOW, PIX), BF),
            shape((DEEP, 2 * C), BF),
            shape((6 * C, 2 * C), BF),
            shape((2 * C, 6 * C), BF),
        ),
        scratch_shapes=[pltpu.VMEM((5, C, C), BF), pltpu.SemaphoreType.DMA((6,))],
        compiler_params=params,
        cost_estimate=cost(1 << 29),
        name="weights",
    )(
        *(
            pltpu.with_memory_space_constraint(x, pltpu.HBM)
            for x in (cot, wide, conv_t, up_t, ws, w_temporal)
        )
    )
    other = swap_cores(own)
    other, wide_v = lax.optimization_barrier((other, wide_v))
    base = jnp.where(
        core == 0, jnp.concatenate([own, other], axis=1), jnp.concatenate([other, own], axis=1)
    ).reshape(FRAMES * LOW, C)
    tied, base = lax.optimization_barrier((cot, base))
    even, odd = (lax.ppermute(tied, "space", swap_pairs(count, first)) for first in (0, 1))
    near = jnp.concatenate(
        [lax.ppermute(base, BOTH, hop_pairs(count, hop)) for hop in (1, 2)], axis=0
    )
    far = swap_cores(near)

    big, direct, act, slope1 = pl.pallas_call(
        prepare_kernel,
        out_shape=(
            shape((n_own, C), BF),
            shape((FRAMES * LOW, C), F32),
            shape((n_own, C), BF),
            shape((n_own, C), F32),
        ),
        scratch_shapes=[
            pltpu.VMEM((FRAMES, WIDE, C), BF),
            pltpu.VMEM((FRAMES * PIX // 2, DEEP), BF),
        ],
        compiler_params=params,
        cost_estimate=cost(1 << 29),
        name="prepare",
    )(base, wide_v, deep, up_t_v, cot_v)
    res, gt_send, gt_keep, d2, slope2 = pl.pallas_call(
        forward_kernel,
        out_shape=(
            shape((n_own, C), BF),
            shape((5 * C // 2, C), BF),
            shape((5 * C // 2, C), F32),
            shape((n_own, C), BF),
            shape((2, n_own, C), F32),
        ),
        scratch_shapes=[
            pltpu.VMEM((5 * n_own, C), BF),
            pltpu.VMEM((4 * FRAMES, WIDE, C), BF),
            pltpu.VMEM((4 * FRAMES * PIX // 2, DEEP), BF),
        ],
        compiler_params=params,
        cost_estimate=cost(1 << 30),
        name="forward",
    )(near, far, wide_v, deep, act, time, cot_v, big)
    send, keep, every = pl.pallas_call(
        backward_kernel,
        out_shape=(
            shape((TAPS * C // 2, C), BF),
            shape((TAPS * C // 2, C), F32),
            shape((FRAMES * LOW, TAPS * C), BF),
        ),
        scratch_shapes=[pltpu.VMEM((FRAMES, LT, C), F32)],
        compiler_params=params,
        cost_estimate=cost(1 << 29),
        name="backward",
    )(even, odd, d2, slope1, slope2, base, conv_t_v, time_t)
    sum_space = keep + swap_cores(send).astype(F32)
    low_send, low_keep = pl.pallas_call(
        late_kernel,
        out_shape=(shape((FRAMES, LCOLS, C), F32),) * 2,
        compiler_params=params,
        cost_estimate=cost(1 << 27),
        name="late",
    )(every, ws_v, direct)

    grad_base = low_keep + swap_cores(low_send)
    halves = []
    sum_time = gt_keep + swap_cores(gt_send).astype(F32)
    for value, levels in ((sum_time, 0), (sum_space, 1)):
        halves.append(reduce_chips(value, count, core, at, levels))
    time_half, space_half = halves
    grad_spatial, grad_temporal = pl.pallas_call(
        output_kernel,
        out_shape=(shape((TAPS * C, C), F32), shape((5 * C, C), F32)),
        compiler_params=params,
        name="output",
    )(space_half, swap_cores(space_half), time_half, swap_cores(time_half))
    return (
        res.reshape(cotangent.shape),
        grad_base.reshape(base_latent.shape),
        grad_spatial.reshape(3, 3, C, C),
        grad_temporal.reshape(5, C, C),
    )


def solution(mesh):
    rows = P(("groups", "space"), "tm", None, None)
    return jax.shard_map(
        local,
        mesh=mesh,
        in_specs=(rows, rows, P(), P()),
        out_specs=(rows, rows, P("groups", None, None, None), P("groups", None, None)),
        check_vma=False,
    )
```

```python
import jax
import jax.numpy as jnp
import numpy as np
from jax import lax
from jax.experimental import pallas as pl
from jax.experimental.pallas import tpu as pltpu
from jax.sharding import PartitionSpec as P

BF = jnp.bfloat16
F32 = jnp.float32
C = 128
FRAMES = 4
ROWS = 4
COLS = 48
LROWS = 2
LCOLS = 12
PIX = ROWS * COLS
LOW = LROWS * LCOLS
TAPS = 9
LT = TAPS * LOW
GROUP = 2 * PIX
BOTH = ("space", "tm")
EXT = ROWS + 2
WIDE = 3 * EXT * COLS
DEEP = 12 * C


def up_matrix(n):
    m = np.zeros((4 * n, n))
    for k in range(n):
        lo, hi = max(k - 1, 0), min(k + 1, n - 1)
        for j, (a, at) in enumerate(((0.375, lo), (0.125, lo), (0.125, hi), (0.375, hi))):
            m[4 * k + j, at] += a
            m[4 * k + j, k] += 1.0 - a
    return m


def moved(m, tap):
    out = np.zeros_like(m)
    for i in range(m.shape[0]):
        if 0 <= i + tap - 1 < m.shape[0]:
            out[i] = m[i + tap - 1]
    return out


def constants():
    rows, cols = up_matrix(LROWS), up_matrix(LCOLS)
    tall = np.pad(rows, ((1, 1), (0, 0)))
    wide = np.stack(
        [
            np.concatenate(
                [np.kron(tall[core * ROWS : core * ROWS + EXT], moved(cols, b)) for b in range(3)]
            )
            for core in range(2)
        ]
    )
    up = np.kron(rows, cols).reshape(2, PIX, LOW)
    conv = np.concatenate(
        [np.kron(moved(rows, a), moved(cols, b)) for a in range(3) for b in range(3)], axis=1
    ).reshape(2, PIX, LT)
    as_bf = lambda m: jnp.asarray(m, BF)
    return as_bf(wide), as_bf(up.transpose(0, 2, 1)), as_bf(conv.transpose(0, 2, 1))


def dot(a, b, dims=((1,), (0,))):
    return lax.dot_general(a, b, (dims, ((), ())), preferred_element_type=F32)


def lanes(parts):
    return jnp.concatenate(parts, axis=1)


def weights_kernel(
    cot_h, wide_h, conv_t_h, up_t_h, ws_h, wt_h, ws, cot, wide, conv_t, up_t, deep, time, time_t, wt, sems
):
    core = lax.axis_index("tm")
    copies = [
        pltpu.make_async_copy(src, dst, sems.at[i])
        for i, (src, dst) in enumerate(
            (
                (ws_h, ws),
                (wt_h, wt),
                (cot_h, cot),
                (wide_h.at[core], wide),
                (up_t_h.at[core], up_t),
                (conv_t_h.at[core], conv_t),
            )
        )
    ]
    for copy in copies:
        copy.start()
    for copy in copies:
        copy.wait()
    zero = jnp.zeros((C, C), BF)
    for b in range(3):
        for d in range(4):
            here = slice((b * 4 + d) * C, (b * 4 + d + 1) * C)
            deep[here, :C] = ws[3 * d + b] if d < 3 else zero
            deep[here, C:] = ws[3 * (d - 1) + b] if d > 0 else zero
    for k in range(6):
        here = slice(k * C, (k + 1) * C)
        time[here, :C] = wt[k] if k < 5 else zero
        time[here, C:] = wt[k - 1] if k > 0 else zero
        time_t[:C, here] = wt[4 - k] if k < 5 else zero
        time_t[C:, here] = wt[5 - k] if k > 0 else zero


def prepare_kernel(base, wide, deep, up_t, cot, big, direct, act, slope1, u3, lhs):
    frames = [base[f * LOW : (f + 1) * LOW, :] for f in range(FRAMES)]
    pre = conv_space(frames, wide, deep, u3, lhs)[0]
    sig = jax.nn.sigmoid(pre)
    one = (pre * sig).astype(BF)
    slope = sig * (1.0 + pre * (1.0 - sig))
    for f in range(FRAMES):
        here = slice(f * PIX, (f + 1) * PIX)
        act[here, :] = image_order(one, f)
        slope1[here, :] = image_order(slope, f)
        big[here, :] = u3[f, (EXT + 1) * COLS : (EXT + 1) * COLS + PIX, :]
    both = dot(up_t[...], lanes([cot[f * PIX : (f + 1) * PIX, :] for f in range(FRAMES)]))
    for f in range(FRAMES):
        direct[f * LOW : (f + 1) * LOW, :] = both[:, f * C : (f + 1) * C]


def conv_space(base_rows, wide, weights, u3, lhs):
    count = len(base_rows)
    for f in range(0, count, 2):
        both = dot(wide[...], lanes(base_rows[f : f + 2])).astype(BF)
        u3[f] = both[:, :C]
        u3[f + 1] = both[:, C:]
    for f in range(count):
        for q in range(2):
            to = (2 * f + q) * COLS
            for b in range(3):
                for d in range(4):
                    frm = (b * EXT + 2 * q + d) * COLS
                    block = b * 4 + d
                    lhs[to : to + COLS, block * C : (block + 1) * C] = u3[f, frm : frm + COLS, :]
    rows = count * PIX // 2
    return [
        dot(lhs[first : first + 2 * PIX, :], weights[...]) for first in range(0, rows, 2 * PIX)
    ]


def image_order(pairs, f):
    out = []
    for q in range(2):
        here = slice((2 * f + q) * COLS, (2 * f + q + 1) * COLS)
        out += [pairs[here, :C], pairs[here, C:]]
    return jnp.concatenate(out, axis=0)


def forward_kernel(
    near, far, wide, deep, act_own, time, cot, big, res, gt_send, gt_keep, d2, slope2, act, u3, lhs
):
    core = lax.axis_index("tm")
    at = lax.axis_index("space")
    count = lax.axis_size("space")
    size = FRAMES * LOW
    before = jnp.where(core == 0, near[...], far[...])
    after = jnp.where(core == 0, far[...], near[...])
    none = jnp.zeros((size, C), BF)
    blocks = (
        jnp.where(at >= 2, before[size:], none),
        jnp.where(at >= 1, before[:size], none),
        jnp.where(at + 1 < count, after[:size], none),
        jnp.where(at + 2 < count, after[size:], none),
    )
    frames = [block[f * LOW : (f + 1) * LOW] for block in blocks for f in range(FRAMES)]
    for k, pre in enumerate(conv_space(frames, wide, deep, u3, lhs)):
        one = (pre * jax.nn.sigmoid(pre)).astype(BF)
        for f in range(FRAMES):
            lo = (FRAMES * (k if k < 2 else k + 1) + f) * PIX
            act[lo : lo + PIX, :] = image_order(one, f)

    def group_of(p):
        if p in (4, 5):
            return act_own[(p - 4) * GROUP : (p - 3) * GROUP, :]
        return act[p * GROUP : (p + 1) * GROUP, :]

    def window(first):
        return lanes([group_of(first + k) for k in range(6)])

    def time_conv(first):
        pre = dot(window(first), time[...])
        sig = jax.nn.sigmoid(pre)
        return pre, sig, sig * (1.0 + pre * (1.0 - sig))

    pre, sig, slope = time_conv(2)
    extra = pre * sig
    for p in range(2):
        here = slice(p * GROUP, (p + 1) * GROUP)
        part = slice(p * C, (p + 1) * C)
        res[here, :] = (big[here, :].astype(F32) + extra[:, part]).astype(BF)
        d2[here, :] = (cot[here, :].astype(F32) * slope[:, part]).astype(BF)
    for side, first in ((0, 0), (1, 4)):
        slope = time_conv(first)[2]
        for p in range(2):
            slope2[side, p * GROUP : (p + 1) * GROUP, :] = slope[:, p * C : (p + 1) * C]

    outer = dot(window(2), lanes([d2[:GROUP, :], d2[GROUP:, :]]), ((0,), (0,)))
    grads = jnp.concatenate(
        [
            outer[t * C : (t + 1) * C, :C] + outer[(t + 1) * C : (t + 2) * C, C:]
            for t in range(5)
        ],
        axis=0,
    )
    halve(grads, core, gt_send, gt_keep)


def halve(grads, core, send, keep):
    rows = grads.shape[0] // 2
    send[...] = jnp.where(core == 0, grads[rows:], grads[:rows]).astype(send.dtype)
    keep[...] = jnp.where(core == 0, grads[:rows], grads[rows:])


def backward_kernel(
    even, odd, d2, slope1, slope2, base, conv_t, time_t, send, keep, every, dsc,
):
    core = lax.axis_index("tm")
    at = lax.axis_index("space")
    count = lax.axis_size("space")
    is_even = at % 2 == 0
    zeros = jnp.zeros((FRAMES * PIX, C), F32)

    def outside(first, second, inside, side):
        got = jnp.where(is_even, first[...], second[...]).astype(F32)
        return jnp.where(inside, got * slope2[side], zeros).astype(BF)

    before = outside(odd, even, at > 0, 0)
    after = outside(even, odd, at < count - 1, 1)
    window = lanes(
        [before[:GROUP], before[GROUP:], d2[:GROUP, :], d2[GROUP:, :], after[:GROUP], after[GROUP:]]
    )
    back = dot(window, time_t[...], ((1,), (1,)))
    for p in range(2):
        lo = p * GROUP
        d1 = (back[:, p * C : (p + 1) * C] * slope1[lo : lo + GROUP, :]).astype(BF)
        small = dot(conv_t[...], lanes([d1[:PIX], d1[PIX:]]))
        dsc[2 * p] = small[:, :C]
        dsc[2 * p + 1] = small[:, C:]
    every[...] = lanes(
        [dsc[:, k * LOW : (k + 1) * LOW, :].reshape(FRAMES * LOW, C).astype(BF) for k in range(TAPS)]
    )
    space = dot(base[...], every[...], ((0,), (0,)))
    halve(
        jnp.concatenate([space[:, k * C : (k + 1) * C] for k in range(TAPS)], axis=0),
        core,
        send,
        keep,
    )


def late_kernel(every, ws, direct, low_send, low_keep):
    core = lax.axis_index("tm")
    total = dot(every[...], lanes([ws[k] for k in range(TAPS)]), ((1,), (1,))) + direct[...]
    for f in range(FRAMES):
        upper = total[f * LOW : f * LOW + LCOLS, :]
        lower = total[f * LOW + LCOLS : (f + 1) * LOW, :]
        low_send[f] = jnp.where(core == 0, lower, upper)
        low_keep[f] = jnp.where(core == 0, upper, lower)


def output_kernel(space_half, space_rest, time_half, time_rest, space, time):
    core = lax.axis_index("tm")
    for half, rest, out in ((space_half, space_rest, space), (time_half, time_rest, time)):
        rows = half.shape[0]
        out[:rows] = jnp.where(core == 0, half[...], rest[...]).astype(F32)
        out[rows:] = jnp.where(core == 0, rest[...], half[...]).astype(F32)


def full(pairs, total):
    sources, targets = {a for a, _ in pairs}, {b for _, b in pairs}
    return pairs + list(
        zip(
            [i for i in range(total) if i not in sources],
            [i for i in range(total) if i not in targets],
        )
    )


def hop_pairs(count, hop):
    pairs = []
    for s in range(count):
        pairs.append((2 * s, 2 * (s + hop)) if s + hop < count else (2 * s, 2 * s + 1))
        pairs.append((2 * s + 1, 2 * (s - hop) + 1) if s - hop >= 0 else (2 * s + 1, 2 * s))
    return pairs


def swap_pairs(count, first):
    pairs = []
    for i in range(first, count - 1, 2):
        pairs += [(i, i + 1), (i + 1, i)]
    return full(pairs, count)


def swap_cores(value):
    return lax.ppermute(value, "tm", [(0, 1), (1, 0)])


def reduce_chips(value, count, core, at, levels):
    bits = count.bit_length() - 1
    if count != 1 << bits:
        return lax.psum(value, "space").astype(BF)
    plain = list(range(bits))
    orders = [plain, plain[-1:] + plain[:-1]]

    def pairs_of(step):
        pairs = []
        for s in range(count):
            for c in range(2):
                pairs.append((2 * s + c, 2 * (s ^ (1 << orders[c][step])) + c))
        return pairs

    def bit_of(step):
        return jnp.where(core == 0, (at >> orders[0][step]) & 1, (at >> orders[1][step]) & 1)

    levels = min(levels, bits)
    for step in range(levels):
        halves = value.reshape(2, value.shape[0] // 2, C)
        bit = bit_of(step)
        out = lax.dynamic_index_in_dim(halves, 1 - bit, 0, False).astype(BF)
        mine = lax.dynamic_index_in_dim(halves, bit, 0, False)
        value = mine + lax.ppermute(out, BOTH, pairs_of(step)).astype(F32)
    for step in range(levels, bits):
        out = value.astype(BF)
        value = out.astype(F32) + lax.ppermute(out, BOTH, pairs_of(step)).astype(F32)
    value = value.astype(BF)
    for step in reversed(range(levels)):
        got = lax.ppermute(value, BOTH, pairs_of(step))
        value = jnp.where(
            bit_of(step) == 0,
            jnp.concatenate([value, got], axis=0),
            jnp.concatenate([got, value], axis=0),
        )
    return value


def local(base_latent, cotangent, w_spatial, w_temporal):
    core = lax.axis_index("tm")
    at = lax.axis_index("space")
    count = lax.axis_size("space")
    wide, up_t, conv_t = constants()
    ws = w_spatial.reshape(TAPS, C, C)
    cot = cotangent.reshape(FRAMES * PIX, C)
    own = base_latent.reshape(FRAMES, LCOLS, C)
    shape = jax.ShapeDtypeStruct
    n_own = FRAMES * PIX
    params = pltpu.CompilerParams(vmem_limit_bytes=32 << 20)
    vmem = pl.BlockSpec(memory_space=pltpu.VMEM)
    hbm = pl.BlockSpec(memory_space=pltpu.HBM)
    cost = lambda flops: pl.CostEstimate(flops=flops, bytes_accessed=2 << 20, transcendentals=0)
    ws_v, cot_v, wide_v, conv_t_v, up_t_v, deep, time, time_t = pl.pallas_call(
        weights_kernel,
        in_specs=[pl.BlockSpec(memory_space=pltpu.HBM)] * 6,
        out_shape=(
            shape((TAPS, C, C), BF),
            shape((n_own, C), BF),
            shape((WIDE, LOW), BF),
            shape((LT, PIX), BF),
            shape((LOW, PIX), BF),
            shape((DEEP, 2 * C), BF),
            shape((6 * C, 2 * C), BF),
            shape((2 * C, 6 * C), BF),
        ),
        scratch_shapes=[pltpu.VMEM((5, C, C), BF), pltpu.SemaphoreType.DMA((6,))],
        compiler_params=params,
        cost_estimate=cost(1 << 29),
        name="weights",
    )(
        *(
            pltpu.with_memory_space_constraint(x, pltpu.HBM)
            for x in (cot, wide, conv_t, up_t, ws, w_temporal)
        )
    )
    other = swap_cores(own)
    other, wide_v = lax.optimization_barrier((other, wide_v))
    base = jnp.where(
        core == 0, jnp.concatenate([own, other], axis=1), jnp.concatenate([other, own], axis=1)
    ).reshape(FRAMES * LOW, C)
    tied, base = lax.optimization_barrier((cot, base))
    even, odd = (lax.ppermute(tied, "space", swap_pairs(count, first)) for first in (0, 1))
    near = jnp.concatenate(
        [lax.ppermute(base, BOTH, hop_pairs(count, hop)) for hop in (1, 2)], axis=0
    )
    far = swap_cores(near)

    big, direct, act, slope1 = pl.pallas_call(
        prepare_kernel,
        out_shape=(
            shape((n_own, C), BF),
            shape((FRAMES * LOW, C), F32),
            shape((n_own, C), BF),
            shape((n_own, C), F32),
        ),
        scratch_shapes=[
            pltpu.VMEM((FRAMES, WIDE, C), BF),
            pltpu.VMEM((FRAMES * PIX // 2, DEEP), BF),
        ],
        compiler_params=params,
        cost_estimate=cost(1 << 29),
        name="prepare",
    )(base, wide_v, deep, up_t_v, cot_v)
    res, gt_send, gt_keep, d2, slope2 = pl.pallas_call(
        forward_kernel,
        out_shape=(
            shape((n_own, C), BF),
            shape((5 * C // 2, C), BF),
            shape((5 * C // 2, C), F32),
            shape((n_own, C), BF),
            shape((2, n_own, C), F32),
        ),
        scratch_shapes=[
            pltpu.VMEM((5 * n_own, C), BF),
            pltpu.VMEM((4 * FRAMES, WIDE, C), BF),
            pltpu.VMEM((4 * FRAMES * PIX // 2, DEEP), BF),
        ],
        compiler_params=params,
        cost_estimate=cost(1 << 30),
        name="forward",
    )(near, far, wide_v, deep, act, time, cot_v, big)
    send, keep, every = pl.pallas_call(
        backward_kernel,
        out_shape=(
            shape((TAPS * C // 2, C), BF),
            shape((TAPS * C // 2, C), F32),
            shape((FRAMES * LOW, TAPS * C), BF),
        ),
        scratch_shapes=[pltpu.VMEM((FRAMES, LT, C), F32)],
        compiler_params=params,
        cost_estimate=cost(1 << 29),
        name="backward",
    )(even, odd, d2, slope1, slope2, base, conv_t_v, time_t)
    sum_space = keep + swap_cores(send).astype(F32)
    sum_space, every = lax.optimization_barrier((sum_space, every))
    low_send, low_keep = pl.pallas_call(
        late_kernel,
        out_shape=(shape((FRAMES, LCOLS, C), F32),) * 2,
        compiler_params=params,
        cost_estimate=cost(1 << 27),
        name="late",
    )(every, ws_v, direct)

    grad_base = low_keep + swap_cores(low_send)
    halves = []
    sum_time = gt_keep + swap_cores(gt_send).astype(F32)
    for value, levels in ((sum_time, 0), (sum_space, 1)):
        halves.append(reduce_chips(value, count, core, at, levels))
    time_half, space_half = halves
    grad_spatial, grad_temporal = pl.pallas_call(
        output_kernel,
        out_shape=(shape((TAPS * C, C), F32), shape((5 * C, C), F32)),
        compiler_params=params,
        name="output",
    )(space_half, swap_cores(space_half), time_half, swap_cores(time_half))
    return (
        res.reshape(cotangent.shape),
        grad_base.reshape(base_latent.shape),
        grad_spatial.reshape(3, 3, C, C),
        grad_temporal.reshape(5, C, C),
    )


def solution(mesh):
    rows = P(("groups", "space"), "tm", None, None)
    return jax.shard_map(
        local,
        mesh=mesh,
        in_specs=(rows, rows, P(), P()),
        out_specs=(rows, rows, P("groups", None, None, None), P("groups", None, None)),
        check_vma=False,
    )
```
